32 devices in a mesh: row: 4 (over y, x), col: 2 (over core), head: 4 (over z).
Axes of the slice: x: 2, y: 2, z: 4, core: 2. Of those that a mesh axis runs over, the one named last changes fastest.
Arguments:
- queries: bfloat16 [192, 64, 1024], P('row', 'col', 'head'), may hold values from -16 to 16
- keys: bfloat16 [192, 64, 1024], P('row', 'col', 'head'), may hold values from -16 to 16
- values: bfloat16 [192, 64, 1024], P('row', 'col', 'head'), may hold values from -16 to 16
- positions: int32 [2, 192, 64], P(None, 'row', 'col'), may hold values from 0 to 192, as said below
- conv_weight: float32 [9, 1024], P(None, 'head'), may hold values from -2 to 2
- norm_gain: float32 [1024], P('head'), may hold values from 0.5 to 1.5
- norm_bias: float32 [1024], P('head'), may hold values from -3 to 3
Outputs:
- normed: bfloat16 [192, 64, 1024], P('row', 'col', 'head')
The draws below stay inside these ranges and needn't reach their ends.
Inputs may be any that keep to these rules, and one draw needn't show every extreme that they name: positions[0] depends only on the grid row and positions[1] only on the grid column; each starts at 0 on the first grid line, rises by 0, 1 or 2 from one line to the next, and ends at 192 (rows) or 64 (columns).
All inputs are finite; a program needn't handle non-finite values.
Results may differ from the reference program's by a relative error of at most 0.0055.
Values may be sent and summed in bfloat16 or wider, within the bound.
A program may use at most 128 MiB of HBM per device.

```python
import math
import jax
import jax.numpy as jnp
from jax import lax

HEADS = 16
HD = 64
D = 1024
AGR = 4
AGC = 1
PR = 12
PC = 32
TR = 48
TC = 32
NR = 192
NC = 64
AGENTS = 32
N_ROW = 4
N_COL = 2


def position_grid(key):
    row_jitter = jax.random.randint(jax.random.fold_in(key, 101), (NR,), 0, 2)
    col_jitter = jax.random.randint(jax.random.fold_in(key, 102), (NC,), 0, 2)
    row_line = jnp.arange(NR, dtype=jnp.int32)
    col_line = jnp.arange(NC, dtype=jnp.int32)
    row_jitter = jnp.where(row_line == 0, 0, jnp.where(row_line == NR - 1, 1, row_jitter))
    col_jitter = jnp.where(col_line == 0, 0, jnp.where(col_line == NC - 1, 1, col_jitter))
    row_index = (row_line + row_jitter).astype(jnp.int32)
    col_index = (col_line + col_jitter).astype(jnp.int32)
    return jnp.stack([jnp.broadcast_to(row_index[:, None], (NR, NC)), jnp.broadcast_to(col_index[None, :], (NR, NC))]).astype(jnp.int32)


def draw_positions(key, part):
    return position_grid(key)


def smooth_field(key, channels, amplitude):
    wave_key = jax.random.fold_in(key, 201)
    key_rows, key_cols, key_phase = jax.random.split(wave_key, 3)
    freq_rows = jax.random.uniform(key_rows, (8,), jnp.float32, -4.0, 4.0)
    freq_cols = jax.random.uniform(key_cols, (8,), jnp.float32, -4.0, 4.0)
    phases = jax.random.uniform(key_phase, (8,), jnp.float32, 0.0, 2.0 * math.pi)
    row_pos = jnp.arange(NR, dtype=jnp.float32) / NR
    col_pos = jnp.arange(NC, dtype=jnp.float32) / NC
    wave_arg = 2.0 * math.pi * (row_pos[:, None, None] * freq_rows + col_pos[None, :, None] * freq_cols) + phases
    wave_basis = jnp.cos(wave_arg)
    return amplitude * jnp.einsum('ijw,wc->ijc', wave_basis, channels) / math.sqrt(8.0)


def query_channels(key):
    return jax.random.normal(jax.random.fold_in(key, 301), (8, D), jnp.float32)


def key_channels(key):
    return 0.7 * query_channels(key) + 0.7 * jax.random.normal(jax.random.fold_in(key, 302), (8, D), jnp.float32)


def value_channels(key):
    return jax.random.normal(jax.random.fold_in(key, 303), (8, D), jnp.float32)


def draw_queries(key, part):
    field = smooth_field(key, query_channels(key), 1.7)
    rough_key = jax.random.fold_in(key, 401)
    result = field + jax.random.normal(rough_key, (NR, NC, D), jnp.float32)
    return jnp.clip(result, -16.0, 16.0).astype(jnp.bfloat16)


def draw_keys(key, part):
    field = smooth_field(key, key_channels(key), 1.7)
    rough_key = jax.random.fold_in(key, 411)
    result = field + jax.random.normal(rough_key, (NR, NC, D), jnp.float32)
    return jnp.clip(result, -16.0, 16.0).astype(jnp.bfloat16)


def draw_values(key, part):
    field = smooth_field(key, value_channels(key), 1.7)
    rough_key = jax.random.fold_in(key, 421)
    channel_ramp = jnp.arange(D, dtype=jnp.float32) / (D - 1)
    rough_part = jax.random.normal(rough_key, (NR, NC, D), jnp.float32)
    result = (field + rough_part) * (0.5 * jnp.power(jnp.float32(4.0), channel_ramp))
    return jnp.clip(result, -16.0, 16.0).astype(jnp.bfloat16)


def levels(stream_key, dims, cuts, least, top_value):
    loudness = 1.0
    for position, blocks in cuts:
        heights = jax.random.uniform(jax.random.fold_in(jax.random.fold_in(stream_key, 6), position), (blocks,), jnp.float32, least / len(cuts), top_value / len(cuts))
        loudness = loudness * jnp.repeat(jnp.exp(heights), dims[position] // blocks).reshape((-1,) + (1,) * (len(dims) - 1 - position))
    return loudness


def bell_draw(stream_key, shape, spread, reach, cuts=(), held_as=jnp.bfloat16):
    level = levels(stream_key, shape, cuts, -0.22, 0.18) if cuts else 1.0
    values = jax.random.normal(stream_key, shape, jnp.float32) * spread * level
    return jnp.minimum(jnp.maximum(values, -reach), reach).astype(held_as)


def setup_inputs(seed: int = 0) -> dict:
    key_list = jax.random.split(jax.random.key(seed), 8)
    queries = draw_queries(jax.random.fold_in(key_list[7], 71), 0)
    keys = draw_keys(jax.random.fold_in(key_list[7], 71), 0)
    values = draw_values(jax.random.fold_in(key_list[7], 71), 0)
    positions = draw_positions(jax.random.fold_in(key_list[7], 71), 0)
    conv_weight = bell_draw(key_list[4], (9, D), 9 ** -0.5, 2.0, ((1, 4),), jnp.float32)
    norm_gain = jnp.clip(1.0 + 0.1 * jax.random.normal(key_list[5], (D,), jnp.float32), 0.5, 1.5)
    norm_bias = bell_draw(key_list[6], (D,), 0.5, 3.0, ((0, 4),), jnp.float32)
    return dict(queries=queries, keys=keys, values=values, positions=positions, conv_weight=conv_weight, norm_gain=norm_gain, norm_bias=norm_bias)


epsilon = 1e-05

def rotate_pairs(segment, angles):
    quarter = segment.shape[-1] // 2
    cosine = jnp.cos(angles)[..., None, :]
    sines = jnp.sin(angles)[..., None, :]
    lower = segment[..., :quarter]
    upper = segment[..., quarter:]
    return jnp.concatenate([lower * cosine - upper * sines, lower * sines + upper * cosine], -1)

def rotary(inputs, positions, head_size):
    full_shape = inputs.shape
    head_count = full_shape[-1] // head_size
    quarter = head_size // 4
    half_size = head_size // 2
    frequency = jnp.power(jnp.float32(100.0), -jnp.arange(quarter, dtype=jnp.float32) / quarter)
    row_angles = positions[0].astype(jnp.float32)[..., None] * frequency
    col_angles = positions[1].astype(jnp.float32)[..., None] * frequency
    unpacked = inputs.astype(jnp.float32).reshape(full_shape[:-1] + (head_count, head_size))
    turned = jnp.concatenate([rotate_pairs(unpacked[..., :half_size], row_angles), rotate_pairs(unpacked[..., half_size:], col_angles)], -1)
    return turned.reshape(full_shape).astype(jnp.bfloat16)

def reference(queries, keys, values, positions, conv_weight, norm_gain, norm_bias):
    score_scale = 1.0 / math.sqrt(HD)
    zero = jnp.zeros((), jnp.int32)
    tile_ids = jnp.arange(N_ROW * N_COL, dtype=jnp.int32)
    padded = jnp.pad(values, ((1, 1), (1, 1), (0, 0)))

    def take_tile(array, tile_index, extra):
        tile_row = (tile_index // N_COL).astype(jnp.int32)
        tile_col = (tile_index % N_COL).astype(jnp.int32)
        return lax.dynamic_slice(array, (tile_row * TR, tile_col * TC, zero), (TR + extra, TC + extra, array.shape[-1]))

    def take_positions(tile_index):
        tile_row = (tile_index // N_COL).astype(jnp.int32)
        tile_col = (tile_index % N_COL).astype(jnp.int32)
        return lax.dynamic_slice(positions, (zero, tile_row * TR, tile_col * TC), (2, TR, TC))

    def pool_tile(tile_index):
        turned = rotary(take_tile(queries, tile_index, 0), take_positions(tile_index), HD)
        cells = turned.astype(jnp.float32).reshape(AGR, PR, AGC, PC, D).mean(axis=(1, 3))
        return cells.reshape(AGR * AGC, D).astype(jnp.bfloat16)
    agents = lax.map(pool_tile, tile_ids).reshape(AGENTS, D)
    agent_heads = agents.astype(jnp.float32).reshape(AGENTS, HEADS, HD)

    def agent_partials(tile_index):
        turned = rotary(take_tile(keys, tile_index, 0), take_positions(tile_index), HD)
        turned = turned.astype(jnp.float32).reshape(TR * TC, HEADS, HD)
        tile_values = take_tile(values, tile_index, 0).astype(jnp.float32).reshape(TR * TC, HEADS, HD)
        scores = jnp.einsum('ahd,thd->hat', agent_heads, turned) * score_scale
        highest = scores.max(-1)
        exponent = jnp.exp(scores - highest[..., None])
        totals = exponent.sum(-1)
        weights = exponent.astype(jnp.bfloat16).astype(jnp.float32)
        numerator = jnp.einsum('hat,thd->had', weights, tile_values)
        return (highest, totals, numerator)
    tile_peaks, tile_totals, tile_numers = lax.map(agent_partials, tile_ids)
    overall = tile_peaks.max(0)
    factor = jnp.exp(tile_peaks - overall)
    totals = (factor * tile_totals).sum(0)
    numerator = (factor[..., None] * tile_numers).sum(0)
    agent_values = (numerator / totals[..., None]).astype(jnp.bfloat16).astype(jnp.float32)

    def output_tile(tile_index):
        turned = rotary(take_tile(queries, tile_index, 0), take_positions(tile_index), HD)
        turned = turned.astype(jnp.float32).reshape(TR * TC, HEADS, HD)
        scores = jnp.einsum('thd,ahd->hta', turned, agent_heads) * score_scale
        probabilities = jax.nn.softmax(scores, -1).astype(jnp.bfloat16).astype(jnp.float32)
        attended = jnp.einsum('hta,had->thd', probabilities, agent_values).reshape(TR, TC, D)
        window = take_tile(padded, tile_index, 2).astype(jnp.float32)
        convolved = jnp.zeros((TR, TC, D), jnp.float32)
        for step_row in range(3):
            for step_col in range(3):
                convolved = convolved + window[step_row:step_row + TR, step_col:step_col + TC] * conv_weight[3 * step_row + step_col]
        summed = attended + convolved
        average = summed.mean(-1, keepdims=True)
        centered = summed - average
        variance = (centered * centered).mean(-1, keepdims=True)
        return (centered * lax.rsqrt(variance + epsilon) * norm_gain + norm_bias).astype(jnp.bfloat16)
    tiles_out = lax.map(output_tile, tile_ids)
    return tiles_out.reshape(N_ROW, N_COL, TR, TC, D).transpose(0, 2, 1, 3, 4).reshape(NR, NC, D)
```

```python
import functools
import math

import jax
import jax.numpy as jnp
from jax import lax
from jax.experimental import pallas as pl
from jax.experimental.pallas import tpu as pltpu
from jax.sharding import PartitionSpec as P

HD = 64
D = 1024
AGR = 4
EPS = 1e-05
F32 = jnp.float32
BF16 = jnp.bfloat16
MESH = pl.DeviceIdType.MESH
NT = (((1,), (1,)), ((), ()))
TN = (((0,), (0,)), ((), ()))


def iota(shape, dim):
    return lax.broadcasted_iota(jnp.int32, shape, dim)


def cos_sin(x):
    n = jnp.floor(x * (2.0 / math.pi) + 0.5)
    r = ((x - n * 1.5703125) - n * 4.837512969970703125e-4) - n * 7.54978995489188216e-8
    z = r * r
    s = ((-1.9515295891e-4 * z + 8.3321608736e-3) * z - 1.6666654611e-1) * z * r + r
    c = ((2.443315711809948e-5 * z - 1.388731625493765e-3) * z + 4.166664568298827e-2) * z * z
    c = c - 0.5 * z + 1.0
    quarter = n.astype(jnp.int32)
    odd = (quarter & 1) == 1
    cosine, sine = jnp.where(odd, s, c), jnp.where(odd, c, s)
    cosine = jnp.where(((quarter + 1) & 2) == 2, -cosine, cosine)
    return cosine, jnp.where((quarter & 2) == 2, -sine, sine)


def kernel(
    n_row, n_col, n_head,
    q_hbm, k_hbm, v_hbm, pos_hbm, w_hbm,
    conv, stat_ref,
    pos_ref, w_ref, q_in, k_in, vp, lh, rh, qt, kt, tabs, tabr, ag, s_ref, pt, mb, sb, hb, own,
    in_sem, ag_s, ag_r, mb_s, mb_r, sb_s, sb_r, hb_s, hb_r, halo_s, halo_r,
):
    rows, cols, chan = q_in.shape
    heads = chan // HD
    patches = rows * cols
    tiles = n_row * n_col
    agents = tiles * AGR
    ha = agents * heads
    row, col, head = lax.axis_index("row"), lax.axis_index("col"), lax.axis_index("head")
    me = row * n_col + col

    def peer(o):
        t = lax.rem(me + o, tiles)
        return (t // n_col, lax.rem(t, n_col), head)

    def head_peer(o):
        return (row, col, lax.rem(head + o, n_head))

    def everyone(ref, send, recv):
        some = ref.at[pl.ds(0, tiles - 1)]
        return pltpu.make_async_remote_copy(
            some, some, send, recv, device_id=peer(1), device_id_type=MESH
        )

    loads = [
        pltpu.make_async_copy(pos_hbm, pos_ref, in_sem.at[3]),
        pltpu.make_async_copy(q_hbm, q_in, in_sem.at[0]),
        pltpu.make_async_copy(k_hbm, k_in, in_sem.at[1]),
        pltpu.make_async_copy(v_hbm, vp.at[pl.ds(1, rows)], in_sem.at[2]),
        pltpu.make_async_copy(w_hbm, w_ref, in_sem.at[4]),
    ]
    for c in loads[:2]:
        c.start()

    barrier = pltpu.get_barrier_semaphore()
    for o in range(1, n_head):
        pl.semaphore_signal(barrier, inc=1, device_id=head_peer(o), device_id_type=MESH)
    for o in range(1, tiles):
        pl.semaphore_signal(barrier, inc=1, device_id=peer(o), device_id_type=MESH)

    step = rows // AGR
    lead = -(-step // 8) * 8
    bins, where = iota((lead + cols, step * cols), 0), iota((lead + cols, step * cols), 1)
    pool = jnp.where(bins < lead, where // cols, where % cols + lead)
    pool = (pool == bins).astype(BF16)

    lane = iota((1, 128), 1)
    freq = jnp.zeros((1, 128), F32)
    for j in range(HD // 4):
        freq = jnp.where(lane % (HD // 4) == j, F32(100.0 ** (-j / (HD // 4))), freq)
    row_lane = (lane % HD) < HD // 2
    src, dst = iota((chan, chan), 0), iota((chan, chan), 1)
    low = (dst % (HD // 2)) < HD // 4
    turn = jnp.where(low & (src - dst == HD // 4), -1.0, 0.0) + jnp.where(
        jnp.logical_not(low) & (dst - src == HD // 4), 1.0, 0.0
    )
    turn = turn.astype(BF16)
    loads[0].wait()
    eye = iota((rows, rows), 0) == iota((rows, rows), 1)
    row_line = jnp.broadcast_to(pos_ref[0, 0:1, :].astype(F32), (rows, rows))
    row_pos = jnp.sum(jnp.where(eye, row_line, 0.0), axis=1, keepdims=True)
    col_pos = pos_ref[1, :, 0:1].astype(F32)
    longest = max(rows, cols)

    def grow(x):
        n = longest - x.shape[0]
        return x if n == 0 else jnp.concatenate([x, jnp.zeros((n, 1), F32)], axis=0)

    cosine, sine = cos_sin(jnp.where(row_lane, grow(row_pos), grow(col_pos)) * freq)
    tabr[0] = jnp.where(row_lane, cosine[:rows], 0.0)
    tabr[1] = jnp.where(row_lane, sine[:rows], 0.0)
    tabs[0] = jnp.where(row_lane, 0.0, cosine[:cols])
    tabs[1] = jnp.where(row_lane, 0.0, sine[:cols])

    def wide(x):
        return jnp.concatenate([x] * (chan // 128), axis=-1)

    def rotate(ref, to, cell):
        x = ref[pl.ds(cell * step, step)].reshape(step * cols, chan)
        crossed = jnp.dot(x, turn, preferred_element_type=F32).reshape(step, cols, chan)
        x = x.astype(F32).reshape(step, cols, chan)
        cosine = wide(tabr[0, pl.ds(cell * step, step)][:, None, :] + tabs[0][None])
        sine = wide(tabr[1, pl.ds(cell * step, step)][:, None, :] + tabs[1][None])
        y = (x * cosine + crossed * sine).astype(BF16)
        to[pl.ds(cell * step * cols, step * cols)] = y.reshape(step * cols, chan)

    loads[1].wait()
    for c in loads[2:]:
        c.start()
    plain, across = [], []
    for cell in range(AGR):
        x = q_in[pl.ds(cell * step, step)].reshape(step * cols, chan)
        sums = jnp.dot(pool, x, preferred_element_type=F32)
        for j, to in enumerate((plain, across)):
            by_row = sums[:step] * wide(tabr[j, pl.ds(cell * step, step)])
            by_col = sums[lead:] * wide(tabs[j])
            to.append(
                jnp.sum(by_row, axis=0, keepdims=True) + jnp.sum(by_col, axis=0, keepdims=True)
            )
    blank = [jnp.zeros((-AGR % 8, chan), F32)] if AGR % 8 else []
    plain = jnp.concatenate(plain + blank, axis=0)
    across = jnp.concatenate(across + blank, axis=0)
    below = (iota(across.shape, 1) % (HD // 2)) < HD // 4
    across = jnp.where(
        below, -pltpu.roll(across, chan - HD // 4, 1), pltpu.roll(across, HD // 4, 1)
    )
    block = ((plain + across) * (1.0 / (step * cols))).astype(BF16).astype(F32)
    ag[me] = (block * (1.0 / math.sqrt(HD)))[:AGR].astype(BF16)

    pl.semaphore_wait(barrier, tiles - 1 + n_head - 1)
    ag_copies = [
        pltpu.make_async_remote_copy(
            ag.at[me], ag.at[me], ag_s, ag_r, device_id=peer(o), device_id_type=MESH
        )
        for o in range(1, tiles)
    ]
    for c in ag_copies:
        c.start()

    edge = 16
    halos = []
    spots = [(-1, 0), (1, 0), (0, -1), (0, 1), (-1, -1), (-1, 1), (1, -1), (1, 1)]
    for i, (dr, dc) in enumerate(spots):
        frm = v_hbm
        if dc == 0:
            frm = v_hbm.at[0 if dr < 0 else rows - 1]
            to = vp.at[rows + 1 if dr < 0 else 0]
        else:
            part = pl.ds(0, edge) if dc < 0 else pl.ds(cols - edge, edge)
            slab = rh if dc < 0 else lh
            if dr == 0:
                frm, to = v_hbm.at[:, part], slab.at[pl.ds(1, rows)]
            else:
                frm = v_hbm.at[0 if dr < 0 else rows - 1, part]
                to = slab.at[rows + 1 if dr < 0 else 0]
        exists = (row + dr >= 0) & (row + dr < n_row) & (col + dc >= 0) & (col + dc < n_col)
        comes = (row - dr >= 0) & (row - dr < n_row) & (col - dc >= 0) & (col - dc < n_col)
        target = (
            jnp.clip(row + dr, 0, n_row - 1), jnp.clip(col + dc, 0, n_col - 1), head,
        )
        c = pltpu.make_async_remote_copy(
            frm, to, halo_s.at[i], halo_r.at[i], device_id=target, device_id_type=MESH
        )
        halos.append((c, exists, comes))
        pl.when(exists)(c.start)

        @pl.when(jnp.logical_not(comes))
        def _():
            to[...] = jnp.zeros(to.shape, BF16)

    for cell in range(AGR):
        rotate(q_in, qt, cell)
    loads[2].wait()
    for cell in range(AGR):
        rotate(k_in, kt, cell)

    loads[3].wait()
    loads[4].wait()
    everyone(ag, ag_s, ag_r).wait()
    mask = (iota((ha, chan), 0) % heads) == iota((ha, chan), 1) // HD
    copies = (iota((ha, agents), 0) // heads == iota((ha, agents), 1)).astype(BF16)
    bd = jnp.dot(copies, ag[...].reshape(agents, chan), preferred_element_type=F32)
    bd = jnp.where(mask, bd, 0.0).astype(BF16)

    chunk = 256
    top = None
    for i in range(patches // chunk):
        s = lax.dot_general(bd, kt[pl.ds(i * chunk, chunk)], NT, preferred_element_type=F32)
        s_ref[:, pl.ds(i * chunk, chunk)] = s
        top = s if top is None else jnp.maximum(top, s)
    peak = jnp.max(top, axis=1, keepdims=True)
    sums = jnp.zeros((ha, chunk), F32)
    numer = jnp.zeros((ha, chan), F32)
    for i in range(patches // chunk):
        e = jnp.exp(s_ref[:, pl.ds(i * chunk, chunk)] - peak)
        sums = sums + e
        v = vp[pl.ds(1 + i * (chunk // cols), chunk // cols)].reshape(chunk, chan)
        numer = numer + jnp.dot(e.astype(BF16), v, preferred_element_type=F32)
    total = jnp.sum(sums, axis=1, keepdims=True)
    means = jnp.where(mask, numer / total, 0.0).astype(BF16)
    pick = (iota((agents, ha), 1) // heads == iota((agents, ha), 0)).astype(BF16)
    mb[me] = jnp.dot(pick, means, preferred_element_type=F32).astype(BF16)
    diag = iota((ha, ha), 0) == iota((ha, ha), 1)
    peak_row = jnp.sum(jnp.where(diag, peak, 0.0), axis=0, keepdims=True)
    total_row = jnp.sum(jnp.where(diag, total, 0.0), axis=0, keepdims=True)
    sb[me] = jnp.where(iota((8, ha), 0) == 0, peak_row, total_row)
    merge = []
    for o in range(1, tiles):
        merge.append(pltpu.make_async_remote_copy(
            sb.at[me], sb.at[me], sb_s, sb_r, device_id=peer(o), device_id_type=MESH
        ))
        merge.append(pltpu.make_async_remote_copy(
            mb.at[me], mb.at[me], mb_s, mb_r, device_id=peer(o), device_id_type=MESH
        ))
    for c in merge:
        c.start()

    def query_softmax(i):
        at = pl.ds(pl.multiple_of(i * chunk, chunk), chunk)
        s = lax.dot_general(bd, qt[at], NT, preferred_element_type=F32)
        s = s.reshape(ha // 8, 8, chunk)
        m = jnp.max(s, axis=0)
        shift = heads
        while shift < 8:
            m = jnp.maximum(m, pltpu.roll(m, shift, 0))
            shift *= 2
        p = jnp.exp(s - m[None])
        z = jnp.sum(p, axis=0)
        shift = heads
        while shift < 8:
            z = z + pltpu.roll(z, shift, 0)
            shift *= 2
        p = (p * (1.0 / z)[None]).reshape(ha, chunk)
        pt[at] = p.T.astype(BF16)

    batch = 3 if (patches // chunk) % 3 == 0 else 1

    def query_batch(i, _):
        for j in range(batch):
            query_softmax(i * batch + j)
        return 0

    lax.fori_loop(0, patches // chunk // batch, query_batch, 0)

    for c, exists, comes in halos:
        pl.when(exists)(c.wait_send)
        pl.when(comes)(c.wait_recv)
    part = 2

    def conv_rows(i, _):
        r0 = i * part
        line = [vp[r0 + d].astype(F32) for d in range(part + 2)]
        left = [lh[r0 + d].astype(F32)[edge - 8:] for d in range(part + 2)]
        right = [rh[r0 + d].astype(F32)[:8] for d in range(part + 2)]
        for r in range(part):
            def taps(src, dj):
                acc = src[r] * w_ref[pl.ds(dj, 1)]
                acc = acc + src[r + 1] * w_ref[pl.ds(3 + dj, 1)]
                return acc + src[r + 2] * w_ref[pl.ds(6 + dj, 1)]
            first = jnp.concatenate([taps(left, 0), taps(line, 0)], axis=0)
            first = pltpu.roll(first, 1, 0)[8:]
            last = jnp.concatenate([taps(line, 2), taps(right, 2)], axis=0)
            last = pltpu.roll(last, cols + 7, 0)[:cols]
            conv[r0 + r] = first + taps(line, 1) + last
        return 0

    lax.fori_loop(0, rows // part, conv_rows, 0)

    everyone(sb, sb_s, sb_r).wait()
    everyone(mb, mb_s, mb_r).wait()
    st = sb[...]
    peaks, totals = st[:, 0, :], st[:, 1, :]
    best = jnp.max(peaks, axis=0, keepdims=True)
    weight = jnp.exp(peaks - best) * totals
    weight = weight / jnp.sum(weight, axis=0, keepdims=True)
    group = max(1, min(tiles, 256 // agents))
    spread = iota((group, agents, ha), 2) // heads == iota((group, agents, ha), 1)
    av = jnp.zeros((ha, chan), F32)
    for g in range(0, tiles, group):
        wide = jnp.where(spread, weight[g:g + group, None, :], 0.0).reshape(group * agents, ha)
        high = wide.astype(BF16)
        less = (wide - high.astype(F32)).astype(BF16)
        every = mb[g:g + group].reshape(group * agents, chan)
        av = av + lax.dot_general(high, every, TN, preferred_element_type=F32)
        av = av + lax.dot_general(less, every, TN, preferred_element_type=F32)
    av = jnp.where(mask, av, 0.0).astype(BF16)

    pieces = own.shape[0]
    size = patches // pieces
    blocks = size // 128
    lines = size // cols
    eye = iota((128, 128), 0) == iota((128, 128), 1)
    for p in range(pieces):
        x = jnp.dot(pt[pl.ds(p * size, size)], av, preferred_element_type=F32)
        x = x + conv[pl.ds(p * lines, lines)].reshape(size, chan)
        conv[pl.ds(p * lines, lines)] = x.reshape(lines, cols, chan)
        one = jnp.sum(x, axis=1, keepdims=True)
        two = jnp.sum(x * x, axis=1, keepdims=True)
        for j, what in enumerate((one, two)):
            for b in range(blocks):
                column = what[b * 128:(b + 1) * 128]
                own[p, pl.ds(j * blocks + b, 1)] = jnp.sum(
                    jnp.where(eye, column, 0.0), axis=0, keepdims=True
                )
        for o in range(1, n_head):
            pltpu.make_async_remote_copy(
                own.at[p], hb.at[p, o - 1], hb_s.at[p], hb_r.at[p],
                device_id=head_peer(o), device_id_type=MESH,
            ).start()

    for p in range(pieces):
        pltpu.make_async_remote_copy(
            hb.at[p], hb.at[p], hb_s.at[p], hb_r.at[p],
            device_id=head_peer(1), device_id_type=MESH,
        ).wait()
        t = own[p]
        for o in range(1, n_head):
            t = t + hb[p, o - 1]
        average = t[:blocks] * (1.0 / D)
        variance = t[blocks:] * (1.0 / D) - average * average
        stat_ref[p] = jnp.concatenate([average, lax.rsqrt(variance + EPS)], axis=0)


def normalize(x_ref, stat_ref, gain_ref, bias_ref, out_hbm, obuf, out_sem):
    rows, cols, chan = x_ref.shape
    pieces = stat_ref.shape[0]
    lines = rows // pieces
    blocks = lines * cols // 128
    part = 128 // cols
    gain, bias = gain_ref[...], bias_ref[...]
    outs = []
    for p in range(pieces):
        for b in range(blocks):
            a = jnp.broadcast_to(stat_ref[p, b:b + 1], (128, 128)).T
            g = jnp.broadcast_to(stat_ref[p, blocks + b:blocks + b + 1], (128, 128)).T
            a = jnp.concatenate([a] * (chan // 128), axis=1)
            g = jnp.concatenate([g] * (chan // 128), axis=1)
            at = pl.ds(p * lines + b * part, part)
            y = (x_ref[at].reshape(128, chan) - a) * g * gain + bias
            obuf[at] = y.astype(BF16).reshape(part, cols, chan)
        at = pl.ds(p * lines, lines)
        c = pltpu.make_async_copy(obuf.at[at], out_hbm.at[at], out_sem.at[p])
        c.start()
        outs.append(c)
    for c in outs:
        c.wait()


def shards(n_row, n_col, n_head, queries, keys, values, positions, conv_weight, gain, bias):
    rows, cols, chan = queries.shape
    heads = chan // HD
    tiles = n_row * n_col
    agents = tiles * AGR
    ha = agents * heads
    patches = rows * cols
    pieces = patches // 512
    need = min(56 * 1024 * 1024, 14 * 1024 * 1024 + 4 * ha * tiles * agents * 8)
    hbm = pl.BlockSpec(memory_space=pltpu.HBM)
    vmem = pl.BlockSpec(memory_space=pltpu.VMEM)
    dma = pltpu.SemaphoreType.DMA
    summed, stats = pl.pallas_call(
        functools.partial(kernel, n_row, n_col, n_head),
        out_shape=[pltpu.VMEM((rows, cols, chan), F32), pltpu.VMEM((pieces, 8, 128), F32)],
        in_specs=[hbm] * 5,
        out_specs=[vmem, vmem],
        scratch_shapes=[
            pltpu.VMEM((2, cols, rows), jnp.int32),
            pltpu.VMEM((9, chan), F32),
            pltpu.VMEM((rows, cols, chan), BF16),
            pltpu.VMEM((rows, cols, chan), BF16),
            pltpu.VMEM((rows + 2, cols, chan), BF16),
            pltpu.VMEM((rows + 2, 16, chan), BF16),
            pltpu.VMEM((rows + 2, 16, chan), BF16),
            pltpu.VMEM((patches, chan), BF16),
            pltpu.VMEM((patches, chan), BF16),
            pltpu.VMEM((2, cols, 128), F32),
            pltpu.VMEM((2, rows, 128), F32),
            pltpu.VMEM((tiles, AGR, chan), BF16),
            pltpu.VMEM((ha, patches), F32),
            pltpu.VMEM((patches, ha), BF16),
            pltpu.VMEM((tiles, agents, chan), BF16),
            pltpu.VMEM((tiles, 8, ha), F32),
            pltpu.VMEM((pieces, n_head - 1, 8, 128), F32),
            pltpu.VMEM((pieces, 8, 128), F32),
            dma((5,)), dma, dma, dma, dma, dma, dma, dma((pieces,)), dma((pieces,)), dma((8,)), dma((8,)),
        ],
        compiler_params=pltpu.CompilerParams(
            collective_id=0, has_side_effects=True, vmem_limit_bytes=need
        ),
        name="agent_attention",
    )(*[
        pltpu.with_memory_space_constraint(a, pltpu.HBM)
        for a in (queries, keys, values, positions.transpose(0, 2, 1), conv_weight)
    ])
    return pl.pallas_call(
        normalize,
        out_shape=jax.ShapeDtypeStruct(queries.shape, BF16),
        in_specs=[vmem, vmem, vmem, vmem],
        out_specs=hbm,
        scratch_shapes=[pltpu.VMEM((rows, cols, chan), BF16), dma((pieces,))],
        compiler_params=pltpu.CompilerParams(vmem_limit_bytes=8 * 1024 * 1024),
        name="normalize",
    )(summed, stats, gain.reshape(1, chan), bias.reshape(1, chan))


def solution(mesh):
    grid = P("row", "col", "head")
    in_specs = (grid, grid, grid, P(None, "row", "col"), P(None, "head"), P("head"), P("head"))
    body = functools.partial(shards, mesh.shape["row"], mesh.shape["col"], mesh.shape["head"])
    return jax.shard_map(body, mesh=mesh, in_specs=in_specs, out_specs=grid, check_vma=False)
```

```python
import functools
import math

import jax
import jax.numpy as jnp
from jax import lax
from jax.experimental import pallas as pl
from jax.experimental.pallas import tpu as pltpu
from jax.sharding import PartitionSpec as P

HD = 64
D = 1024
AGR = 4
EPS = 1e-05
PIECE = 512
F32 = jnp.float32
BF16 = jnp.bfloat16
MESH = pl.DeviceIdType.MESH
NT = (((1,), (1,)), ((), ()))
TN = (((0,), (0,)), ((), ()))


def iota(shape, dim):
    return lax.broadcasted_iota(jnp.int32, shape, dim)


def cos_sin(x):
    n = jnp.floor(x * (2.0 / math.pi) + 0.5)
    r = ((x - n * 1.5703125) - n * 4.837512969970703125e-4) - n * 7.54978995489188216e-8
    z = r * r
    s = ((-1.9515295891e-4 * z + 8.3321608736e-3) * z - 1.6666654611e-1) * z * r + r
    c = ((2.443315711809948e-5 * z - 1.388731625493765e-3) * z + 4.166664568298827e-2) * z * z
    c = c - 0.5 * z + 1.0
    quarter = n.astype(jnp.int32)
    odd = (quarter & 1) == 1
    cosine, sine = jnp.where(odd, s, c), jnp.where(odd, c, s)
    cosine = jnp.where(((quarter + 1) & 2) == 2, -cosine, cosine)
    return cosine, jnp.where((quarter & 2) == 2, -sine, sine)


def kernel(
    n_row, n_col, n_head,
    q_hbm, k_hbm, v_hbm, pos_hbm, w_hbm, gain_hbm, bias_hbm,
    out, stat_ref,
    conv, gain_ref, bias_ref, pos_ref, w_ref, q_in, k_in, vp, lh, rh, qt, kt, tabs, tabr, ag, s_ref, pt, mb, sb, hb, own,
    in_sem, ag_s, ag_r, mb_s, mb_r, sb_s, sb_r, hb_s, hb_r, halo_s, halo_r,
):
    rows, cols, chan = q_in.shape
    heads = chan // HD
    patches = rows * cols
    tiles = n_row * n_col
    agents = tiles * AGR
    ha = agents * heads
    row, col, head = lax.axis_index("row"), lax.axis_index("col"), lax.axis_index("head")
    me = row * n_col + col

    def peer(o):
        t = lax.rem(me + o, tiles)
        return (t // n_col, lax.rem(t, n_col), head)

    def head_peer(o):
        return (row, col, lax.rem(head + o, n_head))

    def everyone(ref, send, recv):
        some = ref.at[pl.ds(0, tiles - 1)]
        return pltpu.make_async_remote_copy(
            some, some, send, recv, device_id=peer(1), device_id_type=MESH
        )

    barrier = pltpu.get_barrier_semaphore()
    for o in range(1, tiles):
        pl.semaphore_signal(barrier, inc=1, device_id=peer(o), device_id_type=MESH)
    for o in range(1, n_head):
        pl.semaphore_signal(barrier, inc=1, device_id=head_peer(o), device_id_type=MESH)

    loads = [
        pltpu.make_async_copy(pos_hbm, pos_ref, in_sem.at[3]),
        pltpu.make_async_copy(q_hbm, q_in, in_sem.at[0]),
        pltpu.make_async_copy(k_hbm, k_in, in_sem.at[1]),
        pltpu.make_async_copy(v_hbm, vp.at[pl.ds(1, rows)], in_sem.at[2]),
        pltpu.make_async_copy(w_hbm, w_ref, in_sem.at[4]),
        pltpu.make_async_copy(gain_hbm, gain_ref, in_sem.at[5]),
        pltpu.make_async_copy(bias_hbm, bias_ref, in_sem.at[6]),
    ]
    for c in loads[:2]:
        c.start()

    step = rows // AGR
    lead = -(-step // 8) * 8
    bins, where = iota((lead + cols, step * cols), 0), iota((lead + cols, step * cols), 1)
    pool = jnp.where(bins < lead, where // cols, where % cols + lead)
    pool = (pool == bins).astype(BF16)

    lane = iota((1, 128), 1)
    freq = jnp.zeros((1, 128), F32)
    for j in range(HD // 4):
        freq = jnp.where(lane % (HD // 4) == j, F32(100.0 ** (-j / (HD // 4))), freq)
    row_lane = (lane % HD) < HD // 2
    src, dst = iota((chan, chan), 0), iota((chan, chan), 1)
    low = (dst % (HD // 2)) < HD // 4
    turn = jnp.where(low & (src - dst == HD // 4), -1.0, 0.0) + jnp.where(
        jnp.logical_not(low) & (dst - src == HD // 4), 1.0, 0.0
    )
    turn = turn.astype(BF16)
    loads[0].wait()
    eye = iota((rows, rows), 0) == iota((rows, rows), 1)
    row_line = jnp.broadcast_to(pos_ref[0, 0:1, :].astype(F32), (rows, rows))
    row_pos = jnp.sum(jnp.where(eye, row_line, 0.0), axis=1, keepdims=True)
    col_pos = pos_ref[1, :, 0:1].astype(F32)
    longest = max(rows, cols)

    def grow(x):
        n = longest - x.shape[0]
        return x if n == 0 else jnp.concatenate([x, jnp.zeros((n, 1), F32)], axis=0)

    cosine, sine = cos_sin(jnp.where(row_lane, grow(row_pos), grow(col_pos)) * freq)
    tabr[0] = jnp.where(row_lane, cosine[:rows], 0.0)
    tabr[1] = jnp.where(row_lane, sine[:rows], 0.0)
    tabs[0] = jnp.where(row_lane, 0.0, cosine[:cols])
    tabs[1] = jnp.where(row_lane, 0.0, sine[:cols])

    def wide(x):
        return jnp.concatenate([x] * (chan // 128), axis=-1)

    def rotate(ref, to, cell):
        x = ref[pl.ds(cell * step, step)].reshape(step * cols, chan)
        crossed = jnp.dot(x, turn, preferred_element_type=F32).reshape(step, cols, chan)
        x = x.astype(F32).reshape(step, cols, chan)
        cosine = wide(tabr[0, pl.ds(cell * step, step)][:, None, :] + tabs[0][None])
        sine = wide(tabr[1, pl.ds(cell * step, step)][:, None, :] + tabs[1][None])
        y = (x * cosine + crossed * sine).astype(BF16)
        to[pl.ds(cell * step * cols, step * cols)] = y.reshape(step * cols, chan)

    loads[1].wait()
    for c in loads[2:]:
        c.start()
    plain, across = [], []
    for cell in range(AGR):
        x = q_in[pl.ds(cell * step, step)].reshape(step * cols, chan)
        sums = jnp.dot(pool, x, preferred_element_type=F32)
        for j, to in enumerate((plain, across)):
            by_row = sums[:step] * wide(tabr[j, pl.ds(cell * step, step)])
            by_col = sums[lead:] * wide(tabs[j])
            to.append(
                jnp.sum(by_row, axis=0, keepdims=True) + jnp.sum(by_col, axis=0, keepdims=True)
            )
    blank = [jnp.zeros((-AGR % 8, chan), F32)] if AGR % 8 else []
    plain = jnp.concatenate(plain + blank, axis=0)
    across = jnp.concatenate(across + blank, axis=0)
    below = (iota(across.shape, 1) % (HD // 2)) < HD // 4
    across = jnp.where(
        below, -pltpu.roll(across, chan - HD // 4, 1), pltpu.roll(across, HD // 4, 1)
    )
    block = ((plain + across) * (1.0 / (step * cols))).astype(BF16).astype(F32)
    ag[me] = (block * (1.0 / math.sqrt(HD)))[:AGR].astype(BF16)

    for cell in range(AGR):
        rotate(q_in, qt, cell)
    pl.semaphore_wait(barrier, tiles - 1 + n_head - 1)
    ag_copies = [
        pltpu.make_async_remote_copy(
            ag.at[me], ag.at[me], ag_s, ag_r, device_id=peer(o), device_id_type=MESH
        )
        for o in range(1, tiles)
    ]
    for c in ag_copies:
        c.start()

    edge = 16
    halos = []
    spots = [(-1, 0), (1, 0), (0, -1), (0, 1), (-1, -1), (-1, 1), (1, -1), (1, 1)]
    for i, (dr, dc) in enumerate(spots):
        frm = v_hbm
        if dc == 0:
            frm = v_hbm.at[0 if dr < 0 else rows - 1]
            to = vp.at[rows + 1 if dr < 0 else 0]
        else:
            part = pl.ds(0, edge) if dc < 0 else pl.ds(cols - edge, edge)
            slab = rh if dc < 0 else lh
            if dr == 0:
                frm, to = v_hbm.at[:, part], slab.at[pl.ds(1, rows)]
            else:
                frm = v_hbm.at[0 if dr < 0 else rows - 1, part]
                to = slab.at[rows + 1 if dr < 0 else 0]
        exists = (row + dr >= 0) & (row + dr < n_row) & (col + dc >= 0) & (col + dc < n_col)
        comes = (row - dr >= 0) & (row - dr < n_row) & (col - dc >= 0) & (col - dc < n_col)
        target = (
            jnp.clip(row + dr, 0, n_row - 1), jnp.clip(col + dc, 0, n_col - 1), head,
        )
        c = pltpu.make_async_remote_copy(
            frm, to, halo_s.at[i], halo_r.at[i], device_id=target, device_id_type=MESH
        )
        halos.append((c, exists, comes))
        pl.when(exists)(c.start)

        @pl.when(jnp.logical_not(comes))
        def _():
            to[...] = jnp.zeros(to.shape, BF16)

    loads[2].wait()
    for cell in range(AGR):
        rotate(k_in, kt, cell)

    loads[3].wait()
    loads[4].wait()
    everyone(ag, ag_s, ag_r).wait()
    mask = (iota((ha, chan), 0) % heads) == iota((ha, chan), 1) // HD
    copies = (iota((ha, agents), 0) // heads == iota((ha, agents), 1)).astype(BF16)
    bd = jnp.dot(copies, ag[...].reshape(agents, chan), preferred_element_type=F32)
    bd = jnp.where(mask, bd, 0.0).astype(BF16)

    chunk = 256
    top = None
    for i in range(patches // chunk):
        s = lax.dot_general(bd, kt[pl.ds(i * chunk, chunk)], NT, preferred_element_type=F32)
        s_ref[:, pl.ds(i * chunk, chunk)] = s
        top = s if top is None else jnp.maximum(top, s)
    peak = jnp.max(top, axis=1, keepdims=True)
    sums = jnp.zeros((ha, chunk), F32)
    numer = jnp.zeros((ha, chan), F32)
    for i in range(patches // chunk):
        e = jnp.exp(s_ref[:, pl.ds(i * chunk, chunk)] - peak)
        sums = sums + e
        v = vp[pl.ds(1 + i * (chunk // cols), chunk // cols)].reshape(chunk, chan)
        numer = numer + jnp.dot(e.astype(BF16), v, preferred_element_type=F32)
    total = jnp.sum(sums, axis=1, keepdims=True)
    means = jnp.where(mask, numer / total, 0.0).astype(BF16)
    pick = (iota((agents, ha), 1) // heads == iota((agents, ha), 0)).astype(BF16)
    mb[me] = jnp.dot(pick, means, preferred_element_type=F32).astype(BF16)
    diag = iota((ha, ha), 0) == iota((ha, ha), 1)
    peak_row = jnp.sum(jnp.where(diag, peak, 0.0), axis=0, keepdims=True)
    total_row = jnp.sum(jnp.where(diag, total, 0.0), axis=0, keepdims=True)
    sb[me] = jnp.where(iota((8, ha), 0) == 0, peak_row, total_row)
    merge = []
    for o in range(1, tiles):
        merge.append(pltpu.make_async_remote_copy(
            sb.at[me], sb.at[me], sb_s, sb_r, device_id=peer(o), device_id_type=MESH
        ))
        merge.append(pltpu.make_async_remote_copy(
            mb.at[me], mb.at[me], mb_s, mb_r, device_id=peer(o), device_id_type=MESH
        ))
    for c in merge:
        c.start()

    def query_softmax(i):
        at = pl.ds(pl.multiple_of(i * chunk, chunk), chunk)
        s = lax.dot_general(bd, qt[at], NT, preferred_element_type=F32)
        s = s.reshape(ha // 8, 8, chunk)
        m = jnp.max(s, axis=0)
        shift = heads
        while shift < 8:
            m = jnp.maximum(m, pltpu.roll(m, shift, 0))
            shift *= 2
        p = jnp.exp(s - m[None])
        z = jnp.sum(p, axis=0)
        shift = heads
        while shift < 8:
            z = z + pltpu.roll(z, shift, 0)
            shift *= 2
        p = (p * (1.0 / z)[None]).reshape(ha, chunk)
        pt[at] = p.T.astype(BF16)

    batch = 3 if (patches // chunk) % 3 == 0 else 1

    def query_batch(i, _):
        for j in range(batch):
            query_softmax(i * batch + j)
        return 0

    lax.fori_loop(0, patches // chunk // batch, query_batch, 0)

    for c, exists, comes in halos:
        pl.when(exists)(c.wait_send)
        pl.when(comes)(c.wait_recv)
    part = 2

    def conv_rows(i, _):
        r0 = i * part
        line = [vp[r0 + d].astype(F32) for d in range(part + 2)]
        left = [lh[r0 + d].astype(F32)[edge - 8:] for d in range(part + 2)]
        right = [rh[r0 + d].astype(F32)[:8] for d in range(part + 2)]
        for r in range(part):
            def taps(src, dj):
                acc = src[r] * w_ref[pl.ds(dj, 1)]
                acc = acc + src[r + 1] * w_ref[pl.ds(3 + dj, 1)]
                return acc + src[r + 2] * w_ref[pl.ds(6 + dj, 1)]
            first = jnp.concatenate([taps(left, 0), taps(line, 0)], axis=0)
            first = pltpu.roll(first, 1, 0)[8:]
            last = jnp.concatenate([taps(line, 2), taps(right, 2)], axis=0)
            last = pltpu.roll(last, cols + 7, 0)[:cols]
            conv[r0 + r] = first + taps(line, 1) + last
        return 0

    lax.fori_loop(0, rows // part, conv_rows, 0)

    everyone(sb, sb_s, sb_r).wait()
    everyone(mb, mb_s, mb_r).wait()
    st = sb[...]
    peaks, totals = st[:, 0, :], st[:, 1, :]
    best = jnp.max(peaks, axis=0, keepdims=True)
    weight = jnp.exp(peaks - best) * totals
    weight = weight / jnp.sum(weight, axis=0, keepdims=True)
    group = max(1, min(tiles, 256 // agents))
    spread = iota((group, agents, ha), 2) // heads == iota((group, agents, ha), 1)
    av = jnp.zeros((ha, chan), F32)
    for g in range(0, tiles, group):
        wide = jnp.where(spread, weight[g:g + group, None, :], 0.0).reshape(group * agents, ha)
        high = wide.astype(BF16)
        less = (wide - high.astype(F32)).astype(BF16)
        every = mb[g:g + group].reshape(group * agents, chan)
        av = av + lax.dot_general(high, every, TN, preferred_element_type=F32)
        av = av + lax.dot_general(less, every, TN, preferred_element_type=F32)
    av = jnp.where(mask, av, 0.0).astype(BF16)

    pieces = own.shape[0]
    size = patches // pieces
    blocks = size // 128
    lines = size // cols
    eye = iota((128, 128), 0) == iota((128, 128), 1)
    ones = jnp.ones((16, chan), BF16)

    def combine(p):
        x = jnp.dot(pt[pl.ds(p * size, size)], av, preferred_element_type=F32)
        x = (x + conv[pl.ds(p * lines, lines)].reshape(size, chan)).astype(BF16)
        out[pl.ds(p * lines, lines)] = x.reshape(lines, cols, chan)
        return x

    later = combine(0)
    for p in range(pieces):
        x = later
        if p < pieces - 1:
            later = combine(p + 1)
        for b in range(blocks):
            y = x[b * 128:(b + 1) * 128]
            one = lax.dot_general(ones, y, NT, preferred_element_type=F32)
            two = lax.dot_general(y, y, NT, preferred_element_type=F32)
            own[p, pl.ds(b, 1)] = one[:1]
            own[p, pl.ds(blocks + b, 1)] = jnp.sum(
                jnp.where(eye, two, 0.0), axis=0, keepdims=True
            )
        for o in range(1, n_head):
            pltpu.make_async_remote_copy(
                own.at[p], hb.at[p, o - 1], hb_s.at[p], hb_r.at[p],
                device_id=head_peer(o), device_id_type=MESH,
            ).start()

    loads[5].wait()
    loads[6].wait()
    for p in range(pieces):
        pltpu.make_async_remote_copy(
            hb.at[p], hb.at[p], hb_s.at[p], hb_r.at[p],
            device_id=head_peer(1), device_id_type=MESH,
        ).wait()
        t = own[p]
        for o in range(1, n_head):
            t = t + hb[p, o - 1]
        average = t[:blocks] * (1.0 / D)
        variance = jnp.maximum(t[blocks:] * (1.0 / D) - average * average, 0.0)
        stat_ref[...] = jnp.concatenate([average, lax.rsqrt(variance + EPS)], axis=0)
        if p < pieces - 1:
            normalize_piece(out, out, stat_ref, gain_ref[...], bias_ref[...], p * lines, p * lines)


def normalize_piece(frm, to, stat_ref, gain, bias, start, put):
    cols, chan = frm.shape[1:]
    blocks = stat_ref.shape[0] // 2
    part = 128 // cols
    for b in range(blocks):
        a = jnp.broadcast_to(stat_ref[b:b + 1], (128, 128)).T
        g = jnp.broadcast_to(stat_ref[blocks + b:blocks + b + 1], (128, 128)).T
        a = jnp.concatenate([a] * (chan // 128), axis=1)
        g = jnp.concatenate([g] * (chan // 128), axis=1)
        x = frm[pl.ds(start + b * part, part)].reshape(128, chan).astype(F32)
        y = (x - a) * g * gain + bias
        to[pl.ds(put + b * part, part)] = y.astype(BF16).reshape(part, cols, chan)


def finish(x_ref, stat_ref, gain_ref, bias_ref, out_hbm, obuf, out_sem):
    rows, lines = x_ref.shape[0], obuf.shape[0]
    copies = []
    if rows > lines:
        at = pl.ds(0, rows - lines)
        copies.append(pltpu.make_async_copy(x_ref.at[at], out_hbm.at[at], out_sem.at[0]))
        copies[0].start()
    normalize_piece(x_ref, obuf, stat_ref, gain_ref[...], bias_ref[...], rows - lines, 0)
    copies.append(
        pltpu.make_async_copy(obuf, out_hbm.at[pl.ds(rows - lines, lines)], out_sem.at[1])
    )
    copies[-1].start()
    for c in copies:
        c.wait()


def shards(n_row, n_col, n_head, queries, keys, values, positions, conv_weight, gain, bias):
    rows, cols, chan = queries.shape
    heads = chan // HD
    tiles = n_row * n_col
    agents = tiles * AGR
    ha = agents * heads
    patches = rows * cols
    pieces = patches // PIECE
    rest = 2 * PIECE // 128
    need = min(56 * 1024 * 1024, 16 * 1024 * 1024 + 4 * ha * tiles * agents * 8)
    hbm = pl.BlockSpec(memory_space=pltpu.HBM)
    vmem = pl.BlockSpec(memory_space=pltpu.VMEM)
    dma = pltpu.SemaphoreType.DMA
    summed, stats = pl.pallas_call(
        functools.partial(kernel, n_row, n_col, n_head),
        out_shape=[pltpu.VMEM((rows, cols, chan), BF16), pltpu.VMEM((rest, 128), F32)],
        in_specs=[hbm] * 7,
        out_specs=[vmem, vmem],
        scratch_shapes=[
            pltpu.VMEM((rows, cols, chan), F32),
            pltpu.VMEM((1, chan), F32),
            pltpu.VMEM((1, chan), F32),
            pltpu.VMEM((2, cols, rows), jnp.int32),
            pltpu.VMEM((9, chan), F32),
            pltpu.VMEM((rows, cols, chan), BF16),
            pltpu.VMEM((rows, cols, chan), BF16),
            pltpu.VMEM((rows + 2, cols, chan), BF16),
            pltpu.VMEM((rows + 2, 16, chan), BF16),
            pltpu.VMEM((rows + 2, 16, chan), BF16),
            pltpu.VMEM((patches, chan), BF16),
            pltpu.VMEM((patches, chan), BF16),
            pltpu.VMEM((2, cols, 128), F32),
            pltpu.VMEM((2, rows, 128), F32),
            pltpu.VMEM((tiles, AGR, chan), BF16),
            pltpu.VMEM((ha, patches), F32),
            pltpu.VMEM((patches, ha), BF16),
            pltpu.VMEM((tiles, agents, chan), BF16),
            pltpu.VMEM((tiles, 8, ha), F32),
            pltpu.VMEM((pieces, n_head - 1, rest, 128), F32),
            pltpu.VMEM((pieces, rest, 128), F32),
            dma((7,)), dma, dma, dma, dma, dma, dma, dma((pieces,)), dma((pieces,)), dma((8,)), dma((8,)),
        ],
        compiler_params=pltpu.CompilerParams(
            collective_id=0, has_side_effects=True, vmem_limit_bytes=need
        ),
        name="agent_attention",
    )(*[
        pltpu.with_memory_space_constraint(a, pltpu.HBM)
        for a in (
            queries, keys, values, positions.transpose(0, 2, 1), conv_weight,
            gain.reshape(1, chan), bias.reshape(1, chan),
        )
    ])
    return pl.pallas_call(
        finish,
        out_shape=jax.ShapeDtypeStruct(queries.shape, BF16),
        in_specs=[vmem, vmem, vmem, vmem],
        out_specs=hbm,
        scratch_shapes=[pltpu.VMEM((PIECE // cols, cols, chan), BF16), dma((2,))],
        compiler_params=pltpu.CompilerParams(vmem_limit_bytes=8 * 1024 * 1024),
        name="normalize",
    )(summed, stats, gain.reshape(1, chan), bias.reshape(1, chan))


def solution(mesh):
    grid = P("row", "col", "head")
    in_specs = (grid, grid, grid, P(None, "row", "col"), P(None, "head"), P("head"), P("head"))
    body = functools.partial(shards, mesh.shape["row"], mesh.shape["col"], mesh.shape["head"])
    return jax.shard_map(body, mesh=mesh, in_specs=in_specs, out_specs=grid, check_vma=False)
```

```python
import functools
import math

import jax
import jax.numpy as jnp
from jax import lax
from jax.experimental import pallas as pl
from jax.experimental.pallas import tpu as pltpu
from jax.sharding import PartitionSpec as P

HD = 64
D = 1024
AGR = 4
EPS = 1e-05
PIECE = 512
F32 = jnp.float32
BF16 = jnp.bfloat16
MESH = pl.DeviceIdType.MESH
NT = (((1,), (1,)), ((), ()))
TN = (((0,), (0,)), ((), ()))


def iota(shape, dim):
    return lax.broadcasted_iota(jnp.int32, shape, dim)


def cos_sin(x):
    n = jnp.floor(x * (2.0 / math.pi) + 0.5)
    r = ((x - n * 1.5703125) - n * 4.837512969970703125e-4) - n * 7.54978995489188216e-8
    z = r * r
    s = ((-1.9515295891e-4 * z + 8.3321608736e-3) * z - 1.6666654611e-1) * z * r + r
    c = ((2.443315711809948e-5 * z - 1.388731625493765e-3) * z + 4.166664568298827e-2) * z * z
    c = c - 0.5 * z + 1.0
    quarter = n.astype(jnp.int32)
    odd = (quarter & 1) == 1
    cosine, sine = jnp.where(odd, s, c), jnp.where(odd, c, s)
    cosine = jnp.where(((quarter + 1) & 2) == 2, -cosine, cosine)
    return cosine, jnp.where((quarter & 2) == 2, -sine, sine)


def kernel(
    n_row, n_col, n_head,
    q_hbm, k_hbm, v_hbm, pos_hbm, w_hbm, gain_hbm, bias_hbm,
    out, stat_ref, affine,
    conv, gain_ref, bias_ref, pos_ref, w_ref, q_in, k_in, vp, lh, rh, qt, kt, tabs, tabr, ag, s_ref, pt, mb, sb, hb, own,
    in_sem, ag_s, ag_r, mb_s, mb_r, sb_s, sb_r, hb_s, hb_r, halo_s, halo_r,
):
    rows, cols, chan = q_in.shape
    heads = chan // HD
    patches = rows * cols
    tiles = n_row * n_col
    agents = tiles * AGR
    ha = agents * heads
    row, col, head = lax.axis_index("row"), lax.axis_index("col"), lax.axis_index("head")
    me = row * n_col + col

    def peer(o):
        t = lax.rem(me + o, tiles)
        return (t // n_col, lax.rem(t, n_col), head)

    def head_peer(o):
        return (row, col, lax.rem(head + o, n_head))

    def everyone(ref, send, recv):
        some = ref.at[pl.ds(0, tiles - 1)]
        return pltpu.make_async_remote_copy(
            some, some, send, recv, device_id=peer(1), device_id_type=MESH
        )

    barrier = pltpu.get_barrier_semaphore()
    for o in range(1, tiles):
        pl.semaphore_signal(barrier, inc=1, device_id=peer(o), device_id_type=MESH)
    for o in range(1, n_head):
        pl.semaphore_signal(barrier, inc=1, device_id=head_peer(o), device_id_type=MESH)

    loads = [
        pltpu.make_async_copy(pos_hbm, pos_ref, in_sem.at[3]),
        pltpu.make_async_copy(q_hbm, q_in, in_sem.at[0]),
        pltpu.make_async_copy(k_hbm, k_in, in_sem.at[1]),
        pltpu.make_async_copy(v_hbm, vp.at[pl.ds(1, rows)], in_sem.at[2]),
        pltpu.make_async_copy(w_hbm, w_ref, in_sem.at[4]),
        pltpu.make_async_copy(gain_hbm, gain_ref, in_sem.at[5]),
        pltpu.make_async_copy(bias_hbm, bias_ref, in_sem.at[6]),
    ]
    for c in loads[:2]:
        c.start()

    step = rows // AGR
    lead = -(-step // 8) * 8
    bins, where = iota((lead + cols, step * cols), 0), iota((lead + cols, step * cols), 1)
    pool = jnp.where(bins < lead, where // cols, where % cols + lead)
    pool = (pool == bins).astype(BF16)

    lane = iota((1, 128), 1)
    freq = jnp.zeros((1, 128), F32)
    for j in range(HD // 4):
        freq = jnp.where(lane % (HD // 4) == j, F32(100.0 ** (-j / (HD // 4))), freq)
    row_lane = (lane % HD) < HD // 2
    src, dst = iota((chan, chan), 0), iota((chan, chan), 1)
    low = (dst % (HD // 2)) < HD // 4
    turn = jnp.where(low & (src - dst == HD // 4), -1.0, 0.0) + jnp.where(
        jnp.logical_not(low) & (dst - src == HD // 4), 1.0, 0.0
    )
    turn = turn.astype(BF16)
    loads[0].wait()
    eye = iota((rows, rows), 0) == iota((rows, rows), 1)
    row_line = jnp.broadcast_to(pos_ref[0, 0:1, :].astype(F32), (rows, rows))
    row_pos = jnp.sum(jnp.where(eye, row_line, 0.0), axis=1, keepdims=True)
    col_pos = pos_ref[1, :, 0:1].astype(F32)
    longest = max(rows, cols)

    def grow(x):
        n = longest - x.shape[0]
        return x if n == 0 else jnp.concatenate([x, jnp.zeros((n, 1), F32)], axis=0)

    cosine, sine = cos_sin(jnp.where(row_lane, grow(row_pos), grow(col_pos)) * freq)
    tabr[0] = jnp.where(row_lane, cosine[:rows], 0.0)
    tabr[1] = jnp.where(row_lane, sine[:rows], 0.0)
    tabs[0] = jnp.where(row_lane, 0.0, cosine[:cols])
    tabs[1] = jnp.where(row_lane, 0.0, sine[:cols])

    def wide(x):
        return jnp.concatenate([x] * (chan // 128), axis=-1)

    def rotate(ref, to, cell):
        x = ref[pl.ds(cell * step, step)].reshape(step * cols, chan)
        crossed = jnp.dot(x, turn, preferred_element_type=F32).reshape(step, cols, chan)
        x = x.astype(F32).reshape(step, cols, chan)
        cosine = wide(tabr[0, pl.ds(cell * step, step)][:, None, :] + tabs[0][None])
        sine = wide(tabr[1, pl.ds(cell * step, step)][:, None, :] + tabs[1][None])
        y = (x * cosine + crossed * sine).astype(BF16)
        to[pl.ds(cell * step * cols, step * cols)] = y.reshape(step * cols, chan)

    loads[1].wait()
    for c in loads[2:]:
        c.start()
    plain, across = [], []
    for cell in range(AGR):
        x = q_in[pl.ds(cell * step, step)].reshape(step * cols, chan)
        sums = jnp.dot(pool, x, preferred_element_type=F32)
        for j, to in enumerate((plain, across)):
            by_row = sums[:step] * wide(tabr[j, pl.ds(cell * step, step)])
            by_col = sums[lead:] * wide(tabs[j])
            to.append(
                jnp.sum(by_row, axis=0, keepdims=True) + jnp.sum(by_col, axis=0, keepdims=True)
            )
    blank = [jnp.zeros((-AGR % 8, chan), F32)] if AGR % 8 else []
    plain = jnp.concatenate(plain + blank, axis=0)
    across = jnp.concatenate(across + blank, axis=0)
    below = (iota(across.shape, 1) % (HD // 2)) < HD // 4
    across = jnp.where(
        below, -pltpu.roll(across, chan - HD // 4, 1), pltpu.roll(across, HD // 4, 1)
    )
    block = ((plain + across) * (1.0 / (step * cols))).astype(BF16).astype(F32)
    ag[me] = (block * (1.0 / math.sqrt(HD)))[:AGR].astype(BF16)

    for cell in range(AGR):
        rotate(q_in, qt, cell)
    pl.semaphore_wait(barrier, tiles - 1 + n_head - 1)
    ag_copies = [
        pltpu.make_async_remote_copy(
            ag.at[me], ag.at[me], ag_s, ag_r, device_id=peer(o), device_id_type=MESH
        )
        for o in range(1, tiles)
    ]
    for c in ag_copies:
        c.start()

    edge = 16
    halos = []
    spots = [(-1, 0), (1, 0), (0, -1), (0, 1), (-1, -1), (-1, 1), (1, -1), (1, 1)]
    for i, (dr, dc) in enumerate(spots):
        frm = v_hbm
        if dc == 0:
            frm = v_hbm.at[0 if dr < 0 else rows - 1]
            to = vp.at[rows + 1 if dr < 0 else 0]
        else:
            part = pl.ds(0, edge) if dc < 0 else pl.ds(cols - edge, edge)
            slab = rh if dc < 0 else lh
            if dr == 0:
                frm, to = v_hbm.at[:, part], slab.at[pl.ds(1, rows)]
            else:
                frm = v_hbm.at[0 if dr < 0 else rows - 1, part]
                to = slab.at[rows + 1 if dr < 0 else 0]
        exists = (row + dr >= 0) & (row + dr < n_row) & (col + dc >= 0) & (col + dc < n_col)
        comes = (row - dr >= 0) & (row - dr < n_row) & (col - dc >= 0) & (col - dc < n_col)
        target = (
            jnp.clip(row + dr, 0, n_row - 1), jnp.clip(col + dc, 0, n_col - 1), head,
        )
        c = pltpu.make_async_remote_copy(
            frm, to, halo_s.at[i], halo_r.at[i], device_id=target, device_id_type=MESH
        )
        halos.append((c, exists, comes))
        pl.when(exists)(c.start)

        @pl.when(jnp.logical_not(comes))
        def _():
            to[...] = jnp.zeros(to.shape, BF16)

    loads[2].wait()
    for cell in range(AGR):
        rotate(k_in, kt, cell)

    loads[3].wait()
    loads[4].wait()
    everyone(ag, ag_s, ag_r).wait()
    mask = (iota((ha, chan), 0) % heads) == iota((ha, chan), 1) // HD
    copies = (iota((ha, agents), 0) // heads == iota((ha, agents), 1)).astype(BF16)
    bd = jnp.dot(copies, ag[...].reshape(agents, chan), preferred_element_type=F32)
    bd = jnp.where(mask, bd, 0.0).astype(BF16)

    chunk = 256
    top = None
    for i in range(patches // chunk):
        s = lax.dot_general(bd, kt[pl.ds(i * chunk, chunk)], NT, preferred_element_type=F32)
        s_ref[:, pl.ds(i * chunk, chunk)] = s
        top = s if top is None else jnp.maximum(top, s)
    peak = jnp.max(top, axis=1, keepdims=True)
    sums = jnp.zeros((ha, chunk), F32)
    numer = jnp.zeros((ha, chan), F32)
    for i in range(patches // chunk):
        e = jnp.exp(s_ref[:, pl.ds(i * chunk, chunk)] - peak)
        sums = sums + e
        v = vp[pl.ds(1 + i * (chunk // cols), chunk // cols)].reshape(chunk, chan)
        numer = numer + jnp.dot(e.astype(BF16), v, preferred_element_type=F32)
    total = jnp.sum(sums, axis=1, keepdims=True)
    means = jnp.where(mask, numer / total, 0.0).astype(BF16)
    pick = (iota((agents, ha), 1) // heads == iota((agents, ha), 0)).astype(BF16)
    mb[me] = jnp.dot(pick, means, preferred_element_type=F32).astype(BF16)
    diag = iota((ha, ha), 0) == iota((ha, ha), 1)
    peak_row = jnp.sum(jnp.where(diag, peak, 0.0), axis=0, keepdims=True)
    total_row = jnp.sum(jnp.where(diag, total, 0.0), axis=0, keepdims=True)
    sb[me] = jnp.where(iota((8, ha), 0) == 0, peak_row, total_row)
    merge = []
    for o in range(1, tiles):
        merge.append(pltpu.make_async_remote_copy(
            sb.at[me], sb.at[me], sb_s, sb_r, device_id=peer(o), device_id_type=MESH
        ))
        merge.append(pltpu.make_async_remote_copy(
            mb.at[me], mb.at[me], mb_s, mb_r, device_id=peer(o), device_id_type=MESH
        ))
    for c in merge:
        c.start()

    def query_softmax(i):
        at = pl.ds(pl.multiple_of(i * chunk, chunk), chunk)
        s = lax.dot_general(bd, qt[at], NT, preferred_element_type=F32)
        s = s.reshape(ha // 8, 8, chunk)
        m = jnp.max(s, axis=0)
        shift = heads
        while shift < 8:
            m = jnp.maximum(m, pltpu.roll(m, shift, 0))
            shift *= 2
        p = jnp.exp(s - m[None])
        z = jnp.sum(p, axis=0)
        shift = heads
        while shift < 8:
            z = z + pltpu.roll(z, shift, 0)
            shift *= 2
        p = (p * (1.0 / z)[None]).reshape(ha, chunk)
        pt[at] = p.T.astype(BF16)

    batch = 3 if (patches // chunk) % 3 == 0 else 1

    def query_batch(i, _):
        for j in range(batch):
            query_softmax(i * batch + j)
        return 0

    lax.fori_loop(0, patches // chunk // batch, query_batch, 0)

    for c, exists, comes in halos:
        pl.when(exists)(c.wait_send)
        pl.when(comes)(c.wait_recv)
    part = 2

    def conv_rows(i, _):
        r0 = i * part
        line = [vp[r0 + d].astype(F32) for d in range(part + 2)]
        left = [lh[r0 + d].astype(F32)[edge - 8:] for d in range(part + 2)]
        right = [rh[r0 + d].astype(F32)[:8] for d in range(part + 2)]
        for r in range(part):
            def taps(src, dj):
                acc = src[r] * w_ref[pl.ds(dj, 1)]
                acc = acc + src[r + 1] * w_ref[pl.ds(3 + dj, 1)]
                return acc + src[r + 2] * w_ref[pl.ds(6 + dj, 1)]
            first = jnp.concatenate([taps(left, 0), taps(line, 0)], axis=0)
            first = pltpu.roll(first, 1, 0)[8:]
            last = jnp.concatenate([taps(line, 2), taps(right, 2)], axis=0)
            last = pltpu.roll(last, cols + 7, 0)[:cols]
            conv[r0 + r] = first + taps(line, 1) + last
        return 0

    lax.fori_loop(0, rows // part, conv_rows, 0)

    everyone(sb, sb_s, sb_r).wait()
    everyone(mb, mb_s, mb_r).wait()
    st = sb[...]
    peaks, totals = st[:, 0, :], st[:, 1, :]
    best = jnp.max(peaks, axis=0, keepdims=True)
    weight = jnp.exp(peaks - best) * totals
    weight = weight / jnp.sum(weight, axis=0, keepdims=True)
    group = max(1, min(tiles, 256 // agents))
    spread = iota((group, agents, ha), 2) // heads == iota((group, agents, ha), 1)
    av = jnp.zeros((ha, chan), F32)
    for g in range(0, tiles, group):
        wide = jnp.where(spread, weight[g:g + group, None, :], 0.0).reshape(group * agents, ha)
        high = wide.astype(BF16)
        less = (wide - high.astype(F32)).astype(BF16)
        every = mb[g:g + group].reshape(group * agents, chan)
        av = av + lax.dot_general(high, every, TN, preferred_element_type=F32)
        av = av + lax.dot_general(less, every, TN, preferred_element_type=F32)
    av = jnp.where(mask, av, 0.0).astype(BF16)

    pieces = own.shape[0]
    size = patches // pieces
    blocks = size // 128
    lines = size // cols
    eye = iota((128, 128), 0) == iota((128, 128), 1)
    ones = jnp.ones((16, chan), BF16)

    def combine(p):
        x = jnp.dot(pt[pl.ds(p * size, size)], av, preferred_element_type=F32)
        x = (x + conv[pl.ds(p * lines, lines)].reshape(size, chan)).astype(BF16)
        out[pl.ds(p * lines, lines)] = x.reshape(lines, cols, chan)
        return x

    later = combine(0)
    for p in range(pieces):
        x = later
        if p < pieces - 1:
            later = combine(p + 1)
        for b in range(blocks):
            y = x[b * 128:(b + 1) * 128]
            both = lax.dot_general(
                jnp.concatenate([ones, y], axis=0), y, NT, preferred_element_type=F32
            )
            own[p, pl.ds(b, 1)] = both[:1]
            own[p, pl.ds(blocks + b, 1)] = jnp.sum(
                jnp.where(eye, both[16:], 0.0), axis=0, keepdims=True
            )
        for o in range(1, n_head):
            pltpu.make_async_remote_copy(
                own.at[p], hb.at[p, o - 1], hb_s.at[p], hb_r.at[p],
                device_id=head_peer(o), device_id_type=MESH,
            ).start()

    loads[5].wait()
    loads[6].wait()
    affine[0:1] = gain_ref[...]
    affine[1:2] = bias_ref[...]
    for p in range(pieces):
        pltpu.make_async_remote_copy(
            hb.at[p], hb.at[p], hb_s.at[p], hb_r.at[p],
            device_id=head_peer(1), device_id_type=MESH,
        ).wait()
        t = own[p]
        for o in range(1, n_head):
            t = t + hb[p, o - 1]
        average = t[:blocks] * (1.0 / D)
        variance = jnp.maximum(t[blocks:] * (1.0 / D) - average * average, 0.0)
        stat_ref[...] = jnp.concatenate([average, lax.rsqrt(variance + EPS)], axis=0)
        if p < pieces - 1:
            normalize_piece(out, out, stat_ref, gain_ref[...], bias_ref[...], p * lines, p * lines)


def normalize_piece(frm, to, stat_ref, gain, bias, start, put):
    cols, chan = frm.shape[1:]
    blocks = stat_ref.shape[0] // 2
    part = 128 // cols
    for b in range(blocks):
        a = jnp.broadcast_to(stat_ref[b:b + 1], (128, 128)).T
        g = jnp.broadcast_to(stat_ref[blocks + b:blocks + b + 1], (128, 128)).T
        a = jnp.concatenate([a] * (chan // 128), axis=1)
        g = jnp.concatenate([g] * (chan // 128), axis=1)
        x = frm[pl.ds(start + b * part, part)].reshape(128, chan).astype(F32)
        y = (x - a) * g * gain + bias
        to[pl.ds(put + b * part, part)] = y.astype(BF16).reshape(part, cols, chan)


def finish(x_ref, stat_ref, affine, out_hbm, obuf, out_sem):
    rows, lines = x_ref.shape[0], obuf.shape[0]
    copies = []
    if rows > lines:
        at = pl.ds(0, rows - lines)
        copies.append(pltpu.make_async_copy(x_ref.at[at], out_hbm.at[at], out_sem.at[0]))
        copies[0].start()
    normalize_piece(x_ref, obuf, stat_ref, affine[0:1], affine[1:2], rows - lines, 0)
    copies.append(
        pltpu.make_async_copy(obuf, out_hbm.at[pl.ds(rows - lines, lines)], out_sem.at[1])
    )
    copies[-1].start()
    for c in copies:
        c.wait()


def shards(n_row, n_col, n_head, queries, keys, values, positions, conv_weight, gain, bias):
    rows, cols, chan = queries.shape
    heads = chan // HD
    tiles = n_row * n_col
    agents = tiles * AGR
    ha = agents * heads
    patches = rows * cols
    pieces = patches // PIECE
    rest = 2 * PIECE // 128
    need = min(56 * 1024 * 1024, 16 * 1024 * 1024 + 4 * ha * tiles * agents * 8)
    hbm = pl.BlockSpec(memory_space=pltpu.HBM)
    vmem = pl.BlockSpec(memory_space=pltpu.VMEM)
    dma = pltpu.SemaphoreType.DMA
    summed, stats, affine = pl.pallas_call(
        functools.partial(kernel, n_row, n_col, n_head),
        out_shape=[pltpu.VMEM((rows, cols, chan), BF16), pltpu.VMEM((rest, 128), F32), pltpu.VMEM((2, chan), F32)],
        in_specs=[hbm] * 7,
        out_specs=[vmem, vmem, vmem],
        scratch_shapes=[
            pltpu.VMEM((rows, cols, chan), F32),
            pltpu.VMEM((1, chan), F32),
            pltpu.VMEM((1, chan), F32),
            pltpu.VMEM((2, cols, rows), jnp.int32),
            pltpu.VMEM((9, chan), F32),
            pltpu.VMEM((rows, cols, chan), BF16),
            pltpu.VMEM((rows, cols, chan), BF16),
            pltpu.VMEM((rows + 2, cols, chan), BF16),
            pltpu.VMEM((rows + 2, 16, chan), BF16),
            pltpu.VMEM((rows + 2, 16, chan), BF16),
            pltpu.VMEM((patches, chan), BF16),
            pltpu.VMEM((patches, chan), BF16),
            pltpu.VMEM((2, cols, 128), F32),
            pltpu.VMEM((2, rows, 128), F32),
            pltpu.VMEM((tiles, AGR, chan), BF16),
            pltpu.VMEM((ha, patches), F32),
            pltpu.VMEM((patches, ha), BF16),
            pltpu.VMEM((tiles, agents, chan), BF16),
            pltpu.VMEM((tiles, 8, ha), F32),
            pltpu.VMEM((pieces, n_head - 1, rest, 128), F32),
            pltpu.VMEM((pieces, rest, 128), F32),
            dma((7,)), dma, dma, dma, dma, dma, dma, dma((pieces,)), dma((pieces,)), dma((8,)), dma((8,)),
        ],
        compiler_params=pltpu.CompilerParams(
            collective_id=0, has_side_effects=True, vmem_limit_bytes=need
        ),
        name="agent_attention",
    )(*[
        pltpu.with_memory_space_constraint(a, pltpu.HBM)
        for a in (
            queries, keys, values, positions.transpose(0, 2, 1), conv_weight,
            gain.reshape(1, chan), bias.reshape(1, chan),
        )
    ])
    return pl.pallas_call(
        finish,
        out_shape=jax.ShapeDtypeStruct(queries.shape, BF16),
        in_specs=[vmem, vmem, vmem],
        out_specs=hbm,
        scratch_shapes=[pltpu.VMEM((PIECE // cols, cols, chan), BF16), dma((2,))],
        compiler_params=pltpu.CompilerParams(vmem_limit_bytes=8 * 1024 * 1024),
        name="normalize",
    )(summed, stats, affine)


def solution(mesh):
    grid = P("row", "col", "head")
    in_specs = (grid, grid, grid, P(None, "row", "col"), P(None, "head"), P("head"), P("head"))
    body = functools.partial(shards, mesh.shape["row"], mesh.shape["col"], mesh.shape["head"])
    return jax.shard_map(body, mesh=mesh, in_specs=in_specs, out_specs=grid, check_vma=False)
```
